32 devices in a mesh: rep: 4 (over x, core), col: 8 (over z, y).
Axes of the slice: x: 2, y: 2, z: 4, core: 2. Of those that a mesh axis runs over, the one named last changes fastest.
Arguments:
- tokens_learn: bfloat16 [5120, 1024], P(None, 'rep'), may hold values from -6 to 6
- cotangent: bfloat16 [1024, 27648], P('rep', 'col'), may hold values from -6 to 6
- sample_ids: int32 [4, 256], P('rep'), may hold values from 0 to 7, never falling along the last dimension, each value on 1 to 64 neighbouring positions
- advantage: float32 [4, 8], P('rep'), may hold values from -2 to 2
- up_weight: bfloat16 [5120, 27648], P('rep', 'col'), may hold values from -0.078125 to 0.078125
- first_moment: float32 [5120, 27648], P('rep', 'col'), may hold values from -3 to 3
- second_moment: float32 [5120, 27648], P('rep', 'col'), may hold values from 0.05 to 1
- rollout_rows: bfloat16 [512, 5120], P('rep', 'col'), may hold values from -6 to 6
- down_proj: bfloat16 [5120, 27648], P(None, 'col'), may hold values from -0.0390625 to 0.0390625
- live_lengths: int32 [4, 4], P('rep'), may hold values from 1 to 32, 96 in all within a row
Outputs:
- new_weight: bfloat16 [5120, 27648], P('rep', 'col')
- new_first: float32 [5120, 27648], P('rep', 'col')
- new_second: float32 [5120, 27648], P('rep', 'col')
- rollout_out: bfloat16 [5120, 512], P('col', 'rep')
The draws below stay inside these ranges and needn't reach their ends.
Inputs may be any that keep to these rules, and one draw needn't show every extreme that they name: `sample_ids`: each lane's sample ids never fall along the lane, and each of the 8 samples has 1 to 64 tokens of that lane. `live_lengths`: the 4 lengths of a replica sum to 96, and one of them is 32.
All inputs are finite; a program needn't handle non-finite values.
Results may differ from the reference program's by a relative error of at most 0.019.
Values may be sent and summed in bfloat16 or wider, within the bound.
No kernel may reach another device: no remote copies, remote signals or barrier semaphores. Data moves between devices by JAX's collectives and lax.ppermute only.
A program may use at most 256 MiB of HBM per device.

```python
import math
import jax
import jax.numpy as jnp
import numpy as np
from jax import lax

D = 5120
FF = 27648
TOK_DEV = 256
SAMPLES = 8
SEG_MOST = 64
SEQS = 4
SLOT = 32
ROWS = 128
LIVE = 96
LANES = 4
REPLICAS = 4


def strengthened(result, stream_key, source, target, parts, factor):
    def block_of(position):
        return (jnp.arange(result.shape[position]) // (result.shape[position] // parts)).reshape((-1,) + (1,) * (result.ndim - 1 - position))

    near = jax.random.permutation(stream_key, parts)[block_of(target)]
    other_side = (block_of(target) + parts // 2) % parts
    return jnp.where((block_of(source) == near) | (block_of(source) == other_side), factor * result, result)


def shard_levels(key, dims, split, low, largest):
    factor_of = 1.0
    for position, blocks in split:
        heights = jax.random.uniform(jax.random.fold_in(jax.random.fold_in(key, 6), position), (blocks,), jnp.float32, low / len(split), largest / len(split))
        factor_of = factor_of * jnp.repeat(jnp.exp(heights), dims[position] // blocks).reshape((-1,) + (1,) * (len(dims) - 1 - position))
    return factor_of


def split_up(count, total, reach, slope):
    loads = [(1 << 20) // math.isqrt(grade ** slope) + 1 for grade in range(2, count + 1)]
    surplus, holding = total - reach - (count - 1), [1] * (count - 1)
    while surplus > 0:
        free = [i for i in range(count - 1) if holding[i] < reach]
        mass, remaining = sum([loads[i] for i in free]), surplus
        for i in free:
            addition = min(reach - holding[i], max(1, remaining * loads[i] // mass), surplus)
            holding[i] = holding[i] + addition
            surplus = surplus - addition
    return np.array([reach] + holding)


def uneven(key, number_of, total, limit, slope):
    if number_of == 2:
        one = jax.random.randint(key, (), max(1, total - limit), min(limit, total - 1) + 1)
        return jnp.stack([one, total - one])
    sizes = jnp.asarray(split_up(number_of, total, limit, slope), jnp.int32)
    twos = (number_of - 1) // 2
    donor, receiver = sizes[1:1 + 2 * twos:2], sizes[2:2 + 2 * twos:2]
    slack = jnp.minimum(donor - 1, limit - receiver)
    shifted = jax.random.randint(jax.random.fold_in(key, 1), (twos,), 0, 1 << 20) % (slack + 1)
    sizes = sizes.at[1:1 + 2 * twos:2].set(donor - shifted).at[2:2 + 2 * twos:2].set(receiver + shifted)
    return sizes[jax.random.permutation(jax.random.fold_in(key, 2), number_of)]


def centred(own_key, extent, scale, bound, cuts=(), kind=jnp.bfloat16):
    entries = jax.random.normal(own_key, extent, jnp.float32) * scale
    if len(cuts) > 0:
        entries = shard_levels(own_key, extent, cuts, -0.22, 0.18) * entries
    return jnp.clip(entries, min=-bound, max=bound).astype(kind)


def gaussian_with(own_key, extent, spread, most, split, heavy, kind=jnp.bfloat16):
    array = spread * jax.random.normal(own_key, extent, jnp.float32)
    if split:
        array = array * shard_levels(own_key, extent, split, -0.22, 0.18)
    return jnp.clip(strengthened(array, jax.random.fold_in(own_key, 3), *heavy), -most, most).astype(kind)


def setup_inputs(seed: int = 0) -> dict:
    key_list = jax.random.split(jax.random.key(seed), 11)
    tokens_learn = gaussian_with(key_list[0], (D, LANES * TOK_DEV), 1.0, 6.0, ((1, 4),), (1, 0, 4, 2.0))
    cotangent = centred(key_list[1], (LANES * TOK_DEV, FF), 1.0, 6.0, ((0, 4), (1, 8)))
    sample_ids = jax.vmap(lambda own: jnp.searchsorted(jnp.cumsum(uneven(own, SAMPLES, TOK_DEV, SEG_MOST, 1)), jnp.arange(TOK_DEV), side="right"))(jax.random.split(key_list[2], LANES)).reshape((LANES, TOK_DEV)).astype(jnp.int32)
    advantage = jnp.clip(jax.random.uniform(key_list[3], (LANES, SAMPLES), jnp.float32, -2.0, 2.0) * shard_levels(key_list[3], (LANES, SAMPLES), ((0, 4),), -0.4, 0.0), -2.0, 2.0)
    up_weight = centred(key_list[4], (D, FF), D ** -0.5, 0.078125, ((0, 4), (1, 8)))
    first_moment = centred(key_list[5], (D, FF), 0.3, 3.0, ((0, 4), (1, 8)), jnp.float32)
    second_moment = jnp.clip(jnp.exp(math.log(1.0) - 2.9957323 * jax.random.uniform(key_list[6], (D, FF), jnp.float32) ** shard_levels(key_list[6], (D, FF), ((0, 4), (1, 8)), -0.2, 0.2)), 0.05, 1.0)
    rollout_rows = centred(key_list[7], (REPLICAS * ROWS, D), 1.0, 6.0, ((0, 4), (1, 8)))
    down_proj = centred(key_list[8], (D, FF), FF ** -0.5, 0.0390625, ((1, 8),))
    live_lengths = jax.vmap(lambda own: uneven(own, SEQS, LIVE, SLOT, 1))(jax.random.split(key_list[9], REPLICAS)).reshape((REPLICAS, SEQS)).astype(jnp.int32)
    return {"tokens_learn": tokens_learn, "cotangent": cotangent, "sample_ids": sample_ids, "advantage": advantage, "up_weight": up_weight, "first_moment": first_moment, "second_moment": second_moment, "rollout_rows": rollout_rows, "down_proj": down_proj, "live_lengths": live_lengths}


first_decay = 0.9
second_decay = 0.95
learn_rate = 0.003
decay_weight = 0.1
adam_epsilon = 1e-08
first_bias = 1.0 - math.exp(100.0 * math.log(0.9))
second_bias = 1.0 - math.exp(100.0 * math.log(0.95))

def token_scales(sample_ids, advantage):
    members = (sample_ids[..., :, None] == jnp.arange(advantage.shape[-1], dtype=jnp.int32)).astype(jnp.float32)
    counts = lax.optimization_barrier(jnp.sum(members, axis=-2))
    ratios = advantage / counts
    return lax.optimization_barrier(jnp.sum(members * ratios[..., None, :], axis=-1))

def adam_update(gradient, up_weight, first_moment, second_moment):
    new_first = first_decay * first_moment + (1.0 - first_decay) * gradient
    new_second = second_decay * second_moment + (1.0 - second_decay) * gradient * gradient
    direction = new_first / first_bias / (jnp.sqrt(new_second / second_bias) + adam_epsilon)
    weight_wide = up_weight.astype(jnp.float32)
    new_weight = (weight_wide - learn_rate * (direction + decay_weight * weight_wide)).astype(jnp.bfloat16)
    return (new_weight, new_first, new_second)

def live_rows(live_lengths, rows_each):
    slot_len = rows_each // SEQS
    positions = jnp.arange(rows_each, dtype=jnp.int32)
    which = positions // slot_len
    within = positions % slot_len
    picks = (which[:, None] == jnp.arange(SEQS, dtype=jnp.int32)[None, :]).astype(jnp.int32)
    limits = lax.optimization_barrier(jnp.sum(live_lengths[:, None, :] * picks[None, :, :], axis=-1))
    return (within[None, :] < limits).astype(jnp.float32).reshape(-1)

def wide_dot(left, right):
    return jnp.dot(left.astype(jnp.float32), right.astype(jnp.float32), precision=lax.Precision.HIGHEST, preferred_element_type=jnp.float32)

def reference(tokens_learn, cotangent, sample_ids, advantage, up_weight, first_moment, second_moment, rollout_rows, down_proj, live_lengths):
    lane_count = advantage.shape[0]
    token_scale = token_scales(sample_ids, advantage)
    token_blocks = jnp.transpose(tokens_learn.reshape(D, lane_count, TOK_DEV), (1, 0, 2))
    cotan_blocks = cotangent.reshape(lane_count, TOK_DEV, FF)

    def lane_step(running, lane_items):
        lane_tokens, lane_cotan, lane_scale = lane_items
        scaled = (lane_scale[:, None] * lane_cotan.astype(jnp.float32)).astype(jnp.bfloat16)
        partial_value = wide_dot(lane_tokens, scaled).astype(jnp.bfloat16)
        return (running + partial_value.astype(jnp.float32), None)
    gradient, _ = lax.scan(lane_step, jnp.zeros((D, FF), jnp.float32), (token_blocks, cotan_blocks, token_scale))
    new_weight, new_first, new_second = adam_update(gradient, up_weight, first_moment, second_moment)
    pre_act = wide_dot(rollout_rows, new_weight)
    live_mask = live_rows(live_lengths, ROWS)
    activation = (jax.nn.silu(pre_act) * live_mask[:, None]).astype(jnp.bfloat16)
    rollout_out = wide_dot(down_proj, activation.T).astype(jnp.bfloat16)
    return (new_weight, new_first, new_second, rollout_out)
```

```python
import functools
import math

import jax
import jax.numpy as jnp
from jax import lax
from jax.experimental import pallas as pl
from jax.experimental.pallas import tpu as pltpu
from jax.sharding import PartitionSpec as P

SEQS = 4
LIVE = 96


first_decay = 0.9
second_decay = 0.95
learn_rate = 0.003
decay_weight = 0.1
adam_epsilon = 1e-08
first_bias = 1.0 - math.exp(100.0 * math.log(0.9))
second_bias = 1.0 - math.exp(100.0 * math.log(0.95))
second_root = math.sqrt(second_bias)


def token_scales(sample_ids, advantage):
    members = (sample_ids[..., :, None] == jnp.arange(advantage.shape[-1], dtype=jnp.int32)).astype(
        jnp.float32
    )
    counts = jnp.sum(members, axis=-2)
    ratios = advantage / counts
    return jnp.sum(members * ratios[..., None, :], axis=-1)


def live_picks(lengths, rows_each):
    slot_len = rows_each // SEQS
    before = jnp.cumsum(lengths) - lengths
    rows = jnp.arange(rows_each, dtype=jnp.int32)
    which, within = rows // slot_len, rows % slot_len
    slot = (which[:, None] == jnp.arange(SEQS, dtype=jnp.int32)[None, :]).astype(jnp.int32)
    start = jnp.sum(slot * before[None, :], axis=1)
    limit = jnp.sum(slot * lengths[None, :], axis=1)
    place = jnp.where(within < limit, start + within, -1)
    return (jnp.arange(LIVE, dtype=jnp.int32)[:, None] == place[None, :]).astype(jnp.bfloat16)


def adam_kernel(lanes, chained, *refs):
    refs = list(refs)
    token_refs, scaled_refs = refs[:lanes], refs[lanes : 2 * lanes]
    w_ref, m_ref, v_ref, x_ref = refs[2 * lanes : 2 * lanes + 4]
    new_w, new_m, new_v, keep_ref, send_ref = refs[2 * lanes + 4 + (3 if chained else 0) :]
    scaled = jnp.concatenate([ref[...] for ref in scaled_refs], axis=0)
    high = new_w.shape[0]
    part = 256 if high % 256 == 0 else high
    for top in range(0, high, part):
        span = slice(top, top + part)
        tokens = jnp.concatenate([ref[span, :] for ref in token_refs], axis=1)
        gradient = jnp.dot(tokens, scaled, preferred_element_type=jnp.float32)
        first = first_decay * m_ref[span, :] + (1.0 - first_decay) * gradient
        second = second_decay * v_ref[span, :] + ((1.0 - second_decay) * gradient) * gradient
        new_m[span, :] = first
        new_v[span, :] = second
        size = jnp.sqrt(second) + adam_epsilon * second_root
        wide = w_ref[span, :].astype(jnp.float32)
        step = (learn_rate * second_root / first_bias) * first / size
        new_w[span, :] = ((1.0 - learn_rate * decay_weight) * wide - step).astype(new_w.dtype)
    half = keep_ref.shape[0]
    partial_value = jnp.dot(x_ref[...], new_w[...], preferred_element_type=jnp.float32)
    keep_ref[...] = partial_value[:half].astype(keep_ref.dtype)
    send_ref[...] = partial_value[half:].astype(send_ref.dtype)


def adam_chunk(tokens, scaled, weight, first, second, rows, chain, start, tile):
    lanes, width, high = len(tokens), scaled[0].shape[1], weight.shape[0]
    skip = start // tile
    block = pl.BlockSpec((high, tile), lambda i: (0, i + skip))
    whole = lambda a: pl.BlockSpec(a.shape, lambda i: (0, 0))
    args = [*tokens, *scaled, weight, first, second, rows]
    specs = [whole(t) for t in tokens]
    specs += [pl.BlockSpec((s.shape[0], tile), lambda i: (0, i)) for s in scaled]
    specs += [block, block, block, whole(rows)]
    alias = {}
    for k, c in enumerate(chain or ()):
        alias[len(args)] = k
        args.append(c)
        specs.append(pl.BlockSpec(memory_space=pl.ANY))
    half = rows.shape[0] // 2
    outs = [jax.ShapeDtypeStruct(a.shape, a.dtype) for a in (weight, first, second)]
    outs += [jax.ShapeDtypeStruct((half, width), jnp.bfloat16)] * 2
    return pl.pallas_call(
        functools.partial(adam_kernel, lanes, bool(chain)),
        out_shape=outs,
        grid=(pl.cdiv(width, tile),),
        in_specs=specs,
        out_specs=[block, block, block] + [pl.BlockSpec((half, tile), lambda i: (0, i))] * 2,
        input_output_aliases=alias,
        name="adam_chunk",
        cost_estimate=pl.CostEstimate(
            flops=2 * high * width * (lanes * tokens[0].shape[1] + rows.shape[0]),
            bytes_accessed=high * width * 20,
            transcendentals=high * width,
        ),
        compiler_params=pltpu.CompilerParams(vmem_limit_bytes=40 * 1024 * 1024),
    )(*args)


def xor_pairs(count, bit):
    return [(i, i ^ bit) for i in range(count)]


def column_chunks(columns):
    tile = 256
    if columns % 128 or columns < 4 * tile:
        return [(0, columns)], columns
    tiles = -(-columns // tile)
    first = -(-tiles * 5 // 14)
    edges = [0, first * tile, 2 * first * tile, columns]
    return [(a, b - a) for a, b in zip(edges, edges[1:])], tile


def body(
    reps,
    cols,
    tokens_learn,
    cotangent,
    sample_ids,
    advantage,
    up_weight,
    first_moment,
    second_moment,
    rollout_rows,
    down_proj,
    live_lengths,
):
    rep, col = lax.axis_index("rep"), lax.axis_index("col")
    swap_rep = lambda a, bit: lax.ppermute(a, "rep", xor_pairs(reps, bit))
    swap_col = lambda a, bit: lax.ppermute(a, "col", xor_pairs(cols, bit))
    bits = [1 << k for k in reversed(range(reps.bit_length() - 1))]
    f32, bf16 = jnp.float32, jnp.bfloat16

    features, depth = tokens_learn.shape
    high = features // reps
    blocks = tokens_learn.reshape(reps, high, depth)
    pick = lambda j: lax.dynamic_index_in_dim(blocks, rep ^ j, 0, keepdims=False)
    side = col & 1
    tokens = [pick(0)]
    for j in range(1, reps):
        if j == 1:
            tokens.append(swap_rep(pick(j), j))
        else:
            mine = swap_rep(
                lax.dynamic_index_in_dim(pick(j).reshape(2, high // 2, depth), side, 0, keepdims=False), j
            )
            other = swap_col(mine, 1)
            tokens.append(
                jnp.concatenate(
                    [jnp.where(side == 0, mine, other), jnp.where(side == 0, other, mine)], axis=0
                )
            )

    picks = live_picks(live_lengths[0], rollout_rows.shape[0])
    compact = jnp.dot(picks, rollout_rows, preferred_element_type=f32).astype(bf16)
    for bit in bits:
        compact = jnp.concatenate([compact, swap_rep(compact, bit)], axis=0)
    per = cols // reps
    spread = jnp.zeros_like(compact)
    for j in range(1, reps):
        pairs = [
            (r * cols + r * per + low, r * cols + (r ^ j) * per + low)
            for r in range(reps)
            for low in range(per)
        ]
        spread = spread + lax.ppermute(compact, ("rep", "col"), pairs)
    rows = jnp.where(col // per == rep, compact, spread)
    for k in range(per.bit_length() - 1):
        other = swap_col(rows, 1 << k)
        upper = (col >> k) & 1
        rows = jnp.concatenate(
            [jnp.where(upper == 0, rows, other), jnp.where(upper == 0, other, rows)], axis=1
        )

    token_scale = token_scales(sample_ids, advantage)[0]
    columns = cotangent.shape[1]
    chunks, tile = column_chunks(columns)
    scaled = []
    for start, width in chunks:
        piece = lax.slice_in_dim(cotangent, start, start + width, axis=1)
        lanes = {0: (token_scale[:, None] * piece.astype(f32)).astype(bf16)}
        for bit in bits:
            lanes.update({j | bit: swap_rep(v, bit) for j, v in list(lanes.items())})
        scaled.append([lanes[j] for j in range(reps)])

    chain = None
    total = None
    for (start, width), lanes in zip(chunks, scaled):
        *chain, keep, send = adam_chunk(
            tokens, lanes, up_weight, first_moment, second_moment, rows, chain, start, tile
        )
        got = swap_rep(send, 1)
        value = keep.astype(f32) + got.astype(f32)
        for bit in bits[-2::-1]:
            half = value.shape[0] // 2
            order = value.reshape(-1, LIVE, width)
            count = order.shape[0]
            value = order[: count // 2].reshape(half, width) + swap_rep(
                order[count // 2 :].reshape(half, width).astype(bf16), bit
            ).astype(f32)
        activation = jax.nn.silu(value).astype(bf16)
        term = lax.dot_general(
            lax.slice_in_dim(down_proj, start, start + width, axis=1),
            activation,
            (((1,), (1,)), ((), ())),
            preferred_element_type=f32,
        )
        total = term if total is None else total + term

    held = total.reshape(cols, features // cols, LIVE)
    bit = cols // 2
    while bit:
        pairs = held.reshape(2, bit, features // cols, LIVE)
        upper = (col // bit) & 1
        mine = lax.dynamic_index_in_dim(pairs, upper, 0, keepdims=False)
        theirs = lax.dynamic_index_in_dim(pairs, 1 - upper, 0, keepdims=False)
        held = mine + swap_col(theirs.astype(bf16), bit).astype(f32)
        bit //= 2
    rollout_out = jnp.dot(held[0].astype(bf16), picks, preferred_element_type=f32).astype(bf16)
    return (*chain, rollout_out)


def solution(mesh):
    placed = (
        P(None, "rep"),
        P("rep", "col"),
        P("rep", None),
        P("rep", None),
        P("rep", "col"),
        P("rep", "col"),
        P("rep", "col"),
        P("rep", "col"),
        P(None, "col"),
        P("rep", None),
    )
    return jax.shard_map(
        functools.partial(body, mesh.shape["rep"], mesh.shape["col"]),
        mesh=mesh,
        in_specs=placed,
        out_specs=(P("rep", "col"), P("rep", "col"), P("rep", "col"), P("col", "rep")),
        check_vma=False,
    )
```

```python
import functools
import math

import jax
import jax.numpy as jnp
from jax import lax
from jax.experimental import pallas as pl
from jax.experimental.pallas import tpu as pltpu
from jax.sharding import PartitionSpec as P


SEQS = 4
LIVE = 96


VMEM_ADAM = 40 * 1024 * 1024
VMEM_DOWN = 32 * 1024 * 1024

first_decay = 0.9
second_decay = 0.95
learn_rate = 0.003
decay_weight = 0.1
adam_epsilon = 1e-08
first_bias = 1.0 - math.exp(100.0 * math.log(0.9))
second_bias = 1.0 - math.exp(100.0 * math.log(0.95))
second_root = math.sqrt(second_bias)


def token_scales(sample_ids, advantage):
    members = (sample_ids[..., :, None] == jnp.arange(advantage.shape[-1], dtype=jnp.int32)).astype(
        jnp.float32
    )
    counts = jnp.sum(members, axis=-2)
    ratios = advantage / counts
    return jnp.sum(members * ratios[..., None, :], axis=-1)


def live_picks(lengths, rows_each):
    slot_len = rows_each // SEQS
    slots = jnp.arange(SEQS, dtype=jnp.int32)
    before = jnp.sum(jnp.where(slots[None, :] < slots[:, None], lengths[None, :], 0), axis=1)
    rows = jnp.arange(rows_each, dtype=jnp.int32)
    which, within = rows // slot_len, rows % slot_len
    slot = (which[:, None] == jnp.arange(SEQS, dtype=jnp.int32)[None, :]).astype(jnp.int32)
    start = jnp.sum(slot * before[None, :], axis=1)
    limit = jnp.sum(slot * lengths[None, :], axis=1)
    place = jnp.where(within < limit, start + within, -1)
    return (jnp.arange(LIVE, dtype=jnp.int32)[:, None] == place[None, :]).astype(jnp.bfloat16)


def adam_kernel(lanes, chained, previous, own, *refs):
    refs = list(refs)
    token_refs, scaled_refs = refs[:lanes], refs[lanes : 2 * lanes]
    w_ref, m_ref, v_ref, x_ref = refs[2 * lanes : 2 * lanes + 4]
    refs = refs[2 * lanes + 4 :]
    past_w = refs[0] if chained else None
    new_w, new_m, new_v, *products = refs[3 if chained else 0 :]
    scaled = jnp.concatenate([ref[...] for ref in scaled_refs], axis=0)
    high = new_w.shape[0]
    part = 256 if high % 256 == 0 else high
    for top in range(0, high, part):
        span = slice(top, top + part)
        tokens = jnp.concatenate([ref[span, :] for ref in token_refs], axis=1)
        gradient = jnp.dot(tokens, scaled, preferred_element_type=jnp.float32)
        first = first_decay * m_ref[span, :] + (1.0 - first_decay) * gradient
        second = second_decay * v_ref[span, :] + ((1.0 - second_decay) * gradient) * gradient
        new_m[span, :] = first
        new_v[span, :] = second
        size = jnp.sqrt(second) + adam_epsilon * second_root
        wide = w_ref[span, :].astype(jnp.float32)
        step = (learn_rate * second_root / first_bias) * first / size
        new_w[span, :] = ((1.0 - learn_rate * decay_weight) * wide - step).astype(new_w.dtype)
    for k, source in enumerate(([past_w] if previous else []) + ([new_w] if own else [])):
        keep_ref, send_ref = products
        half = keep_ref.shape[1]
        value = jnp.dot(x_ref[...], source[...], preferred_element_type=jnp.float32)
        keep_ref[k] = value[:half].astype(keep_ref.dtype)
        send_ref[k] = value[half:].astype(send_ref.dtype)


def adam_chunk(tokens, scaled, weight, first, second, rows, chain, start, tile, previous, own):
    lanes, width, high = len(tokens), scaled[0].shape[1], weight.shape[0]
    skip = start // tile
    block = pl.BlockSpec((high, tile), lambda i: (0, i + skip))
    whole = lambda a: pl.BlockSpec(a.shape, lambda i: (0, 0))
    x_arg = rows if rows is not None else jnp.zeros((16, 128), jnp.bfloat16)
    args = [*tokens, *scaled, weight, first, second, x_arg]
    specs = [whole(t) for t in tokens]
    specs += [pl.BlockSpec((s.shape[0], tile), lambda i: (0, i)) for s in scaled]
    specs += [block, block, block, whole(x_arg)]
    alias = {}
    for k, c in enumerate(chain or ()):
        alias[len(args)] = k
        args.append(c)
        if k == 0 and previous:
            back = width // tile
            specs.append(pl.BlockSpec((high, tile), lambda i: (0, i + skip - back)))
        else:
            specs.append(pl.BlockSpec(memory_space=pl.ANY))
    outs = [jax.ShapeDtypeStruct(a.shape, a.dtype) for a in (weight, first, second)]
    out_specs = [block, block, block]
    groups = int(previous) + int(own)
    if groups:
        half = rows.shape[0] // 2
        outs += [jax.ShapeDtypeStruct((groups, half, width), jnp.bfloat16)] * 2
        out_specs += [pl.BlockSpec((groups, half, tile), lambda i: (0, 0, i))] * 2
    return pl.pallas_call(
        functools.partial(adam_kernel, lanes, bool(chain), previous, own),
        out_shape=outs,
        grid=(pl.cdiv(width, tile),),
        in_specs=specs,
        out_specs=out_specs,
        input_output_aliases=alias,
        cost_estimate=pl.CostEstimate(
            flops=2 * high * width * (lanes * tokens[0].shape[1] + groups * LIVE * 4),
            bytes_accessed=high * width * 20,
            transcendentals=high * width,
        ),
        compiler_params=pltpu.CompilerParams(vmem_limit_bytes=VMEM_ADAM),
    )(*args)


def down_kernel(groups, last, *refs):
    where_ref, *refs = refs
    own_refs, other_refs = refs[:groups], refs[groups : 2 * groups]
    first_ref, second_ref = refs[2 * groups : 2 * groups + 2]
    weights = jnp.concatenate([first_ref[...], second_ref[...]], axis=0)
    live = own_refs[0].shape[0]
    total = None
    for k in range(groups):
        width = own_refs[k].shape[1]
        act = jnp.concatenate([own_refs[k][...], other_refs[k][...]], axis=0)
        term = lax.dot_general(
            act,
            weights[:, k * width : (k + 1) * width],
            (((1,), (1,)), ((), ())),
            preferred_element_type=jnp.float32,
        )
        total = term if total is None else total + term
    if last:
        past_ref, own_out, other_out = refs[2 * groups + 2 :]
        total = total + past_ref[...]
        own_out[...] = total[:live].astype(own_out.dtype)
        other_out[...] = total[live:].astype(other_out.dtype)
    else:
        refs[-1][...] = total


def down_part(down_proj, own, other, where, start, past):
    cols = 8
    groups, (live, width) = len(own), own[0].shape
    unit = down_proj.shape[0] // cols // 2
    span = groups * width
    bits = lambda i: (i // 2) + 2 * (i % 2)

    def weight_spec(top):
        if start % span == 0:
            return pl.BlockSpec(
                (unit, span), lambda i, w: ((w[0] ^ (bits(i) + top)) * 2 + w[1], start // span)
            )
        return pl.BlockSpec(
            (pl.Element(unit), pl.Element(span)),
            lambda i, w: (((w[0] ^ (bits(i) + top)) * 2 + w[1]) * unit, start),
        )

    whole = lambda a: pl.BlockSpec(a.shape, lambda i, w: (0, 0))
    args = [*own, *other, down_proj, down_proj]
    specs = [whole(a) for a in (*own, *other)] + [weight_spec(0), weight_spec(4)]
    if past is None:
        outs = jax.ShapeDtypeStruct((2 * live, 8 * unit), jnp.float32)
        out_specs = pl.BlockSpec((2 * live, 2 * unit), lambda i, w: (0, i))
    else:
        args.append(past)
        specs.append(pl.BlockSpec((2 * live, 2 * unit), lambda i, w: (0, i)))
        outs = [jax.ShapeDtypeStruct((live, 8 * unit), jnp.bfloat16)] * 2
        out_specs = [
            pl.BlockSpec((live, 2 * unit), lambda i, w: (0, i)),
            pl.BlockSpec((live, 2 * unit), lambda i, w: (0, bits(i))),
        ]
    return pl.pallas_call(
        functools.partial(down_kernel, groups, past is not None),
        out_shape=outs,
        grid_spec=pltpu.PrefetchScalarGridSpec(
            num_scalar_prefetch=1, grid=(4,), in_specs=specs, out_specs=out_specs
        ),
        cost_estimate=pl.CostEstimate(
            flops=4 * live * 8 * unit * span, bytes_accessed=8 * unit * span * 2, transcendentals=0
        ),
        compiler_params=pltpu.CompilerParams(vmem_limit_bytes=VMEM_DOWN),
    )(where, *args)


def xor_pairs(count, bit):
    return [(i, i ^ bit) for i in range(count)]


def column_chunks(columns):
    tile = 256
    if columns % 128 or columns < 4 * tile:
        return [(0, columns)], columns
    tiles = -(-columns // tile)
    first = -(-tiles * 5 // 14)
    edges = [0, first * tile, 2 * first * tile, columns]
    return [(a, b - a) for a, b in zip(edges, edges[1:])], tile


def inner(
    reps,
    cols,
    tokens_learn,
    cotangent,
    sample_ids,
    advantage,
    up_weight,
    first_moment,
    second_moment,
    rollout_rows,
    down_proj,
    live_lengths,
):
    rep, col = lax.axis_index("rep"), lax.axis_index("col")
    swap_rep = lambda a, bit: lax.ppermute(a, "rep", xor_pairs(reps, bit))
    swap_col = lambda a, bit: lax.ppermute(a, "col", xor_pairs(cols, bit))
    bits = [1 << k for k in reversed(range(reps.bit_length() - 1))]
    f32, bf16 = jnp.float32, jnp.bfloat16

    features, depth = tokens_learn.shape
    high = features // reps
    quarter = high // 4
    blocks = tokens_learn.reshape(reps, 4, quarter, depth)
    part = col & 3

    def piece(j, which):
        return lax.dynamic_slice(blocks, (rep ^ j, which, 0, 0), (1, 1, quarter, depth))[0, 0]

    far = range(2, reps)
    near = lax.dynamic_index_in_dim(blocks, rep ^ 1, 0, keepdims=False).reshape(high, depth)
    pieces = [piece(j, part) for j in far]
    pieces, near, sample_ids, live_lengths = lax.optimization_barrier(
        (pieces, near, sample_ids, live_lengths)
    )
    straight = {}
    for j in far:
        straight[j] = swap_rep(pieces[j - 2], j)
    near = swap_rep(near, 1)

    token_scale = token_scales(sample_ids, advantage)[0]
    columns = cotangent.shape[1]
    chunks, tile = column_chunks(columns)
    scaled = []
    for start, width in chunks:
        own = lax.slice_in_dim(cotangent, start, start + width, axis=1)
        lanes = {0: (token_scale[:, None] * own.astype(f32)).astype(bf16)}
        for bit in bits:
            for j, value in list(lanes.items()):
                lanes[j | bit] = swap_rep(value, bit)
        scaled.append([lanes[j] for j in range(reps)])

    tokens = [lax.dynamic_index_in_dim(blocks, rep, 0, keepdims=False).reshape(high, depth), near]
    for j in far:
        second = swap_col(straight[j], 2)
        third = swap_col(straight[j], 1)
        fourth = swap_col(second, 1)
        got = [straight[j], third, second, fourth]
        tokens.append(jnp.concatenate([lax.select_n(part ^ i, *got) for i in range(4)], axis=0))

    picks = live_picks(live_lengths[0], rollout_rows.shape[0])
    compact = jnp.dot(picks, rollout_rows, preferred_element_type=f32).astype(bf16)
    per = cols // reps
    slabs = [compact]
    for i in range(1, reps):
        slabs.append(swap_col(compact, i * per))
    turn = (col // per) ^ rep
    order = [0]
    for bit in bits:
        order += [j | bit for j in order]
    rows = []
    for j in order:
        slab = lax.select_n(turn ^ j, *slabs)
        rows.append(slab if j == 0 else swap_rep(slab, j))
    rows = jnp.concatenate(rows, axis=0)
    for k in range(per.bit_length() - 1):
        other = swap_col(rows, 1 << k)
        upper = (col >> k) & 1
        rows = jnp.concatenate(
            [jnp.where(upper == 0, rows, other), jnp.where(upper == 0, other, rows)], axis=1
        )

    def reduced(keep, send):
        got = swap_rep(send, 1)
        value = keep.astype(f32) + got.astype(f32)
        for bit in bits[-2::-1]:
            half = value.shape[1] // 2
            got = swap_rep(value[:, half:].astype(bf16), bit)
            value = value[:, :half] + got.astype(f32)
        return jax.nn.silu(value).astype(bf16)

    chain, acts = None, []
    unit = features // cols
    paired = cols == 8 and unit % 128 == 0 and unit % 32 == 0 and len(chunks) == 3
    for index, ((start, width), lanes) in enumerate(zip(chunks, scaled)):
        only = len(chunks) == 1
        previous, own = (not only and index == 1), (only or index > 0)
        *out, = adam_chunk(
            tokens, lanes, up_weight, first_moment, second_moment,
            rows if own or previous else None, chain, start, tile, previous, own,
        )
        chain = out[:3]
        if own:
            act = reduced(*out[3:])
            acts += [act[k] for k in range(act.shape[0])]

    if paired:
        where = jnp.stack([col, rep & 1]).astype(jnp.int32)
        pair = swap_rep(jnp.stack(acts[:2]), 1)
        past = down_part(down_proj, acts[:2], [pair[0], pair[1]], where, 0, None)
        pair = swap_rep(acts[2], 1)
        own, other = down_part(down_proj, acts[2:], [pair], where, chunks[2][0], past)

        def stage(value, bit):
            half = value.shape[1] // 2
            got = swap_col(value[:, half:], bit)
            return (value[:, :half].astype(f32) + got.astype(f32)).astype(bf16)

        for one, two in ((1, 2), (2, 1), (4, 4)):
            own, other = stage(own, one), stage(other, two)
        other = swap_rep(other, 1)
        lower = (rep & 1) == 0
        held = jnp.concatenate([jnp.where(lower, own, other), jnp.where(lower, other, own)], axis=1)
        rollout_out = lax.dot_general(
            held, picks, (((0,), (0,)), ((), ())), preferred_element_type=f32
        ).astype(bf16)
        return (*chain, rollout_out)

    total = None
    for (start, width), act in zip(chunks, acts):
        term = lax.dot_general(
            lax.slice_in_dim(down_proj, start, start + width, axis=1),
            act,
            (((1,), (1,)), ((), ())),
            preferred_element_type=f32,
        )
        total = term if total is None else total + term
    held = total.reshape(cols, unit, LIVE)
    bit = cols // 2
    while bit:
        pairs = held.reshape(2, bit, unit, LIVE)
        upper = (col // bit) & 1
        mine = lax.dynamic_index_in_dim(pairs, upper, 0, keepdims=False)
        theirs = lax.dynamic_index_in_dim(pairs, 1 - upper, 0, keepdims=False)
        held = mine + swap_col(theirs.astype(bf16), bit).astype(f32)
        bit //= 2
    rollout_out = jnp.dot(held[0].astype(bf16), picks, preferred_element_type=f32).astype(bf16)
    return (*chain, rollout_out)


def body(reps, cols, *args):
    return inner(reps, cols, *args)


def solution(mesh):
    placed = (
        P(None, "rep"),
        P("rep", "col"),
        P("rep", None),
        P("rep", None),
        P("rep", "col"),
        P("rep", "col"),
        P("rep", "col"),
        P("rep", "col"),
        P(None, "col"),
        P("rep", None),
    )
    return jax.shard_map(
        functools.partial(body, mesh.shape["rep"], mesh.shape["col"]),
        mesh=mesh,
        in_specs=placed,
        out_specs=(P("rep", "col"), P("rep", "col"), P("rep", "col"), P("col", "rep")),
        check_vma=False,
    )
```

```python
import functools
import math

import jax
import jax.numpy as jnp
from jax import lax
from jax.experimental import pallas as pl
from jax.experimental.pallas import tpu as pltpu
from jax.sharding import PartitionSpec as P


SEQS = 4
LIVE = 96


RESIDENT = ()
VMEM_ADAM = 31 * 1024 * 1024
VMEM_DOWN = 32 * 1024 * 1024

first_decay = 0.9
second_decay = 0.95
learn_rate = 0.003
decay_weight = 0.1
adam_epsilon = 1e-08
first_bias = 1.0 - math.exp(100.0 * math.log(0.9))
second_bias = 1.0 - math.exp(100.0 * math.log(0.95))
second_root = math.sqrt(second_bias)


def token_scales(sample_ids, advantage):
    members = (sample_ids[..., :, None] == jnp.arange(advantage.shape[-1], dtype=jnp.int32)).astype(
        jnp.float32
    )
    counts = jnp.sum(members, axis=-2)
    ratios = advantage / counts
    return jnp.sum(members * ratios[..., None, :], axis=-1)


def live_picks(lengths, rows_each):
    slot_len = rows_each // SEQS
    slots = jnp.arange(SEQS, dtype=jnp.int32)
    before = jnp.sum(jnp.where(slots[None, :] < slots[:, None], lengths[None, :], 0), axis=1)
    rows = jnp.arange(rows_each, dtype=jnp.int32)
    which, within = rows // slot_len, rows % slot_len
    slot = (which[:, None] == jnp.arange(SEQS, dtype=jnp.int32)[None, :]).astype(jnp.int32)
    start = jnp.sum(slot * before[None, :], axis=1)
    limit = jnp.sum(slot * lengths[None, :], axis=1)
    place = jnp.where(within < limit, start + within, -1)
    return (jnp.arange(LIVE, dtype=jnp.int32)[:, None] == place[None, :]).astype(jnp.bfloat16)


def adam_kernel(lanes, chained, previous, own, resident, *refs):
    refs = list(refs)
    token_refs, scaled_refs = refs[:lanes], refs[lanes : 2 * lanes]
    w_ref, m_ref, v_ref, x_ref = refs[2 * lanes : 2 * lanes + 4]
    refs = refs[2 * lanes + 4 :]
    past_w = refs[0] if chained else None
    new_w, new_m, new_v, *products = refs[3 if chained else 0 :]
    scaled = jnp.concatenate([ref[...] for ref in scaled_refs], axis=0)
    high, tile = new_w.shape
    if resident:
        here = pl.ds(pl.multiple_of(pl.program_id(0) * tile, tile), tile)
        w_ref, m_ref, v_ref = w_ref.at[:, here], m_ref.at[:, here], v_ref.at[:, here]
    part = 256 if high % 256 == 0 else high
    for top in range(0, high, part):
        span = slice(top, top + part)
        tokens = jnp.concatenate([ref[span, :] for ref in token_refs], axis=1)
        gradient = jnp.dot(tokens, scaled, preferred_element_type=jnp.float32)
        first = first_decay * m_ref[span, :] + (1.0 - first_decay) * gradient
        second = second_decay * v_ref[span, :] + ((1.0 - second_decay) * gradient) * gradient
        new_m[span, :] = first
        new_v[span, :] = second
        size = jnp.sqrt(second) + adam_epsilon * second_root
        wide = w_ref[span, :].astype(jnp.float32)
        step = (learn_rate * second_root / first_bias) * first / size
        new_w[span, :] = ((1.0 - learn_rate * decay_weight) * wide - step).astype(new_w.dtype)
    for k, source in enumerate(([past_w] if previous else []) + ([new_w] if own else [])):
        keep_ref, send_ref = products
        half = keep_ref.shape[1]
        value = jnp.dot(x_ref[...], source[...], preferred_element_type=jnp.float32)
        keep_ref[k] = value[:half].astype(keep_ref.dtype)
        send_ref[k] = value[half:].astype(send_ref.dtype)


def adam_chunk(tokens, scaled, weight, first, second, rows, chain, start, tile, previous, own, resident):
    lanes, width, high = len(tokens), scaled[0].shape[1], weight.shape[0]
    skip = start // tile
    block = pl.BlockSpec((high, tile), lambda i: (0, i + skip))
    whole = lambda a: pl.BlockSpec(a.shape, lambda i: (0, 0))
    x_arg = rows if rows is not None else jnp.zeros((16, 128), jnp.bfloat16)
    inputs = [weight, first, second]
    if resident:
        inputs = [lax.slice_in_dim(a, start, start + width, axis=1) for a in inputs]
    else:
        inputs = [pltpu.with_memory_space_constraint(a, pltpu.HBM) for a in inputs]
    args = [*tokens, *scaled, *inputs, x_arg]
    specs = [whole(t) for t in tokens]
    specs += [pl.BlockSpec((s.shape[0], tile), lambda i: (0, i)) for s in scaled]
    specs += [pl.BlockSpec(memory_space=pltpu.VMEM) if resident else block] * 3 + [whole(x_arg)]
    alias = {}
    for k, c in enumerate(chain or ()):
        alias[len(args)] = k
        args.append(c)
        if k == 0 and previous:
            back = width // tile
            specs.append(pl.BlockSpec((high, tile), lambda i: (0, i + skip - back)))
        else:
            specs.append(pl.BlockSpec(memory_space=pl.ANY))
    outs = [jax.ShapeDtypeStruct(a.shape, a.dtype) for a in (weight, first, second)]
    out_specs = [block, block, block]
    groups = int(previous) + int(own)
    if groups:
        half = rows.shape[0] // 2
        outs += [jax.ShapeDtypeStruct((groups, half, width), jnp.bfloat16)] * 2
        out_specs += [pl.BlockSpec((groups, half, tile), lambda i: (0, 0, i))] * 2
    return pl.pallas_call(
        functools.partial(adam_kernel, lanes, bool(chain), previous, own, resident),
        out_shape=outs,
        grid=(pl.cdiv(width, tile),),
        in_specs=specs,
        out_specs=out_specs,
        input_output_aliases=alias,
        cost_estimate=pl.CostEstimate(
            flops=2 * high * width * (lanes * tokens[0].shape[1] + groups * LIVE * 4),
            bytes_accessed=high * width * 20,
            transcendentals=high * width,
        ),
        compiler_params=pltpu.CompilerParams(vmem_limit_bytes=VMEM_ADAM),
    )(*args)


def down_kernel(groups, last, *refs):
    where_ref, *refs = refs
    own_refs, other_refs = refs[:groups], refs[groups : 2 * groups]
    first_ref, second_ref = refs[2 * groups : 2 * groups + 2]
    weights = jnp.concatenate([first_ref[...], second_ref[...]], axis=0)
    live = own_refs[0].shape[0]
    total = None
    for k in range(groups):
        width = own_refs[k].shape[1]
        act = jnp.concatenate([own_refs[k][...], other_refs[k][...]], axis=0)
        term = lax.dot_general(
            act,
            weights[:, k * width : (k + 1) * width],
            (((1,), (1,)), ((), ())),
            preferred_element_type=jnp.float32,
        )
        total = term if total is None else total + term
    if last:
        past_ref, own_out, other_out = refs[2 * groups + 2 :]
        total = total + past_ref[...]
        own_out[...] = total[:live].astype(own_out.dtype)
        other_out[...] = total[live:].astype(other_out.dtype)
    else:
        refs[-1][...] = total


def down_part(down_proj, own, other, where, start, past):
    cols = 8
    groups, (live, width) = len(own), own[0].shape
    unit = down_proj.shape[0] // cols // 2
    span = groups * width
    bits = lambda i: (i // 2) + 2 * (i % 2)

    def weight_spec(top):
        if start % span == 0:
            return pl.BlockSpec(
                (unit, span), lambda i, w: ((w[0] ^ (bits(i) + top)) * 2 + w[1], start // span)
            )
        return pl.BlockSpec(
            (pl.Element(unit), pl.Element(span)),
            lambda i, w: (((w[0] ^ (bits(i) + top)) * 2 + w[1]) * unit, start),
        )

    whole = lambda a: pl.BlockSpec(a.shape, lambda i, w: (0, 0))
    args = [*own, *other, down_proj, down_proj]
    specs = [whole(a) for a in (*own, *other)] + [weight_spec(0), weight_spec(4)]
    if past is None:
        outs = jax.ShapeDtypeStruct((2 * live, 8 * unit), jnp.float32)
        out_specs = pl.BlockSpec((2 * live, 2 * unit), lambda i, w: (0, i))
    else:
        args.append(past)
        specs.append(pl.BlockSpec((2 * live, 2 * unit), lambda i, w: (0, i)))
        outs = [jax.ShapeDtypeStruct((live, 8 * unit), jnp.bfloat16)] * 2
        out_specs = [
            pl.BlockSpec((live, 2 * unit), lambda i, w: (0, i)),
            pl.BlockSpec((live, 2 * unit), lambda i, w: (0, bits(i))),
        ]
    return pl.pallas_call(
        functools.partial(down_kernel, groups, past is not None),
        out_shape=outs,
        grid_spec=pltpu.PrefetchScalarGridSpec(
            num_scalar_prefetch=1, grid=(4,), in_specs=specs, out_specs=out_specs
        ),
        cost_estimate=pl.CostEstimate(
            flops=4 * live * 8 * unit * span, bytes_accessed=8 * unit * span * 2, transcendentals=0
        ),
        compiler_params=pltpu.CompilerParams(vmem_limit_bytes=VMEM_DOWN),
    )(where, *args)


def xor_pairs(count, bit):
    return [(i, i ^ bit) for i in range(count)]


def column_chunks(columns):
    tile = 384
    if columns % (3 * tile):
        return [(0, columns)], columns
    width = columns // 3
    return [(k * width, width) for k in range(3)], tile


def inner(
    reps,
    cols,
    tokens_learn,
    cotangent,
    sample_ids,
    advantage,
    up_weight,
    first_moment,
    second_moment,
    rollout_rows,
    down_proj,
    live_lengths,
):
    rep, col = lax.axis_index("rep"), lax.axis_index("col")
    swap_rep = lambda a, bit: lax.ppermute(a, "rep", xor_pairs(reps, bit))
    swap_col = lambda a, bit: lax.ppermute(a, "col", xor_pairs(cols, bit))
    bits = [1 << k for k in reversed(range(reps.bit_length() - 1))]
    f32, bf16 = jnp.float32, jnp.bfloat16

    features, depth = tokens_learn.shape
    high = features // reps
    blocks = tokens_learn.reshape(reps, 2, high // 2, depth)
    side = col & 1
    far = range(2, reps)
    pieces = [lax.dynamic_slice(blocks, (rep ^ j, side, 0, 0), (1, 1, high // 2, depth)) for j in far]
    pieces, blocks, sample_ids, live_lengths = lax.optimization_barrier(
        (pieces, blocks, sample_ids, live_lengths)
    )
    whole_block = lambda j: lax.dynamic_index_in_dim(blocks, rep ^ j, 0, keepdims=False)
    straight = {}
    for j in far:
        straight[j] = swap_rep(pieces[j - 2][0, 0], j)
    near = swap_rep(whole_block(1).reshape(high, depth), 1)

    token_scale = token_scales(sample_ids, advantage)[0]
    columns = cotangent.shape[1]
    chunks, tile = column_chunks(columns)
    scaled = []
    for start, width in chunks:
        own = lax.slice_in_dim(cotangent, start, start + width, axis=1)
        lanes = {0: (token_scale[:, None] * own.astype(f32)).astype(bf16)}
        for bit in bits:
            for j, value in list(lanes.items()):
                lanes[j | bit] = swap_rep(value, bit)
        scaled.append([lanes[j] for j in range(reps)])

    tokens = [whole_block(0).reshape(high, depth), near]
    for j in far:
        second = swap_col(straight[j], 1)
        tokens.append(
            jnp.concatenate([lax.select_n(side ^ i, straight[j], second) for i in range(2)], axis=0)
        )

    picks = live_picks(live_lengths[0], rollout_rows.shape[0])
    compact = jnp.dot(picks, rollout_rows, preferred_element_type=f32).astype(bf16)
    per = cols // reps
    slabs = [compact]
    for i in range(1, reps):
        slabs.append(swap_col(compact, i * per))
    turn = (col // per) ^ rep
    order = [0]
    for bit in bits:
        order += [j | bit for j in order]
    rows = []
    for j in order:
        slab = lax.select_n(turn ^ j, *slabs)
        rows.append(slab if j == 0 else swap_rep(slab, j))
    rows = jnp.concatenate(rows, axis=0)
    for k in range(per.bit_length() - 1):
        other = swap_col(rows, 1 << k)
        upper = (col >> k) & 1
        rows = jnp.concatenate(
            [jnp.where(upper == 0, rows, other), jnp.where(upper == 0, other, rows)], axis=1
        )

    def reduced(keep, send):
        got = swap_rep(send, 1)
        terms = [keep, got]
        for bit in bits[-2::-1]:
            half = terms[0].shape[1] // 2
            send = sum(t[:, half:].astype(f32) for t in terms).astype(bf16)
            terms = [t[:, :half] for t in terms] + [swap_rep(send, bit)]
        value = sum(t.astype(f32) for t in terms)
        return jax.nn.silu(value).astype(bf16)

    chain, acts = None, []
    unit = features // cols
    paired = cols == 8 and unit % 128 == 0 and unit % 32 == 0 and len(chunks) == 3
    for index, ((start, width), lanes) in enumerate(zip(chunks, scaled)):
        only = len(chunks) == 1
        previous, own = (not only and index == 1), (only or index > 0)
        *out, = adam_chunk(
            tokens, lanes, up_weight, first_moment, second_moment,
            rows if own or previous else None, chain, start, tile, previous, own,
            not only and index in RESIDENT,
        )
        chain = out[:3]
        if own:
            act = reduced(*out[3:])
            acts += [act[k] for k in range(act.shape[0])]

    if paired:
        where = jnp.stack([col, rep & 1]).astype(jnp.int32)
        pair = swap_rep(jnp.stack(acts[:2]), 1)
        past = down_part(down_proj, acts[:2], [pair[0], pair[1]], where, 0, None)
        pair = swap_rep(acts[2], 1)
        own, other = down_part(down_proj, acts[2:], [pair], where, chunks[2][0], past)

        def stage(value, bit):
            half = value.shape[1] // 2
            got = swap_col(value[:, half:], bit)
            return (value[:, :half].astype(f32) + got.astype(f32)).astype(bf16)

        for one, two in ((1, 2), (2, 1)):
            own, other = stage(own, one), stage(other, two)
        own, other = jnp.split(stage(jnp.concatenate([own, other], axis=0), 4), 2, axis=0)
        other = swap_rep(other, 1)
        lower = (rep & 1) == 0
        held = jnp.concatenate([jnp.where(lower, own, other), jnp.where(lower, other, own)], axis=1)
        rollout_out = lax.dot_general(
            held, picks, (((0,), (0,)), ((), ())), preferred_element_type=f32
        ).astype(bf16)
        return (*chain, rollout_out)

    total = None
    for (start, width), act in zip(chunks, acts):
        term = lax.dot_general(
            lax.slice_in_dim(down_proj, start, start + width, axis=1),
            act,
            (((1,), (1,)), ((), ())),
            preferred_element_type=f32,
        )
        total = term if total is None else total + term
    held = total.reshape(cols, unit, LIVE)
    bit = cols // 2
    while bit:
        pairs = held.reshape(2, bit, unit, LIVE)
        upper = (col // bit) & 1
        mine = lax.dynamic_index_in_dim(pairs, upper, 0, keepdims=False)
        theirs = lax.dynamic_index_in_dim(pairs, 1 - upper, 0, keepdims=False)
        held = mine + swap_col(theirs.astype(bf16), bit).astype(f32)
        bit //= 2
    rollout_out = jnp.dot(held[0].astype(bf16), picks, preferred_element_type=f32).astype(bf16)
    return (*chain, rollout_out)


def body(reps, cols, *args):
    return inner(reps, cols, *args)


def solution(mesh):
    placed = (
        P(None, "rep"),
        P("rep", "col"),
        P("rep", None),
        P("rep", None),
        P("rep", "col"),
        P("rep", "col"),
        P("rep", "col"),
        P("rep", "col"),
        P(None, "col"),
        P("rep", None),
    )
    return jax.shard_map(
        functools.partial(body, mesh.shape["rep"], mesh.shape["col"]),
        mesh=mesh,
        in_specs=placed,
        out_specs=(P("rep", "col"), P("rep", "col"), P("rep", "col"), P("col", "rep")),
        check_vma=False,
    )
```
